32 devices in a mesh: frames: 4 (over y, x), pix: 8 (over z, core).
Axes of the slice: x: 2, y: 2, z: 4, core: 2. Of those that a mesh axis runs over, the one named last changes fastest.
Arguments:
- intensity: bfloat16 [128, 524288], P('frames', 'pix'), may hold values from -6 to 6
- chi_bin: int32 [524288], P('pix'), may hold values from 0 to 255
- split: float32 [524288], P('pix'), may hold values from 0 to 1
- mask: int32 [524288], P('pix'), may hold values 0 or 1
- tile_row: int32 [4096], P('pix'), may hold values from 0 to 255
Outputs:
- correlation: float32 [256, 2, 128, 256], P('frames', None, 'pix')
The draws below stay inside these ranges and needn't reach their ends.
All inputs are finite; a program needn't handle non-finite values. No bound on the sum of `mask` on one device may be relied on, other than what follows from the above.
Results may differ from the reference program's by a relative error of at most 0.0027.
Values sent between devices are 32-bit elements; how exact they have to be, the bound alone decides.
No kernel may reach another device: no remote copies, remote signals or barrier semaphores. Data moves between devices by JAX's collectives and lax.ppermute only.
A program may use at most 128 MiB of HBM per device.

```python
import math
import jax
import jax.numpy as jnp
from jax import lax

NQ = 256
NCHI = 256
NH = 128
FRAMES = 128
PIX = 524288
TILES = 4096


def draw_tile_row(key, part):
    base_key = jax.random.fold_in(key, 4243)
    order_key, rows_key, pick_key = jax.random.split(base_key, 3)
    cycle_order = jax.random.permutation(order_key, NQ).astype(jnp.int32)
    slots = jax.random.randint(rows_key, (TILES,), 0, NQ - 8).astype(jnp.int32)
    lonely = jax.random.permutation(pick_key, TILES)[:4].astype(jnp.int32)
    slots = slots.at[lonely].set((NQ - 4 + jnp.arange(4)).astype(jnp.int32))
    return cycle_order[slots].astype(jnp.int32)


def plant(result, key, smallest, largest):
    longest = result.shape.index(max(result.shape))
    spots = []
    for shift in (0, 1):
        where = [jax.random.randint(jax.random.fold_in(key, axis), (), 0, length) for axis, length in enumerate(result.shape)]
        where[longest] = (where[longest] + shift) % result.shape[longest]
        spots.append(tuple(where))
    return result.at[spots[0]].set(smallest).at[spots[1]].set(largest)


def shard_levels(own_key, shape, cuts, least, high):
    def one(position, shards_of):
        heights = jax.random.uniform(jax.random.fold_in(jax.random.fold_in(own_key, 6), position), (shards_of,), jnp.float32, least / len(cuts), high / len(cuts))
        return jnp.repeat(jnp.exp(heights), shape[position] // shards_of).reshape((-1,) + (1,) * (len(shape) - position - 1))

    factor_of = one(*cuts[0])
    for cut in cuts[1:]:
        factor_of = factor_of * one(*cut)
    return factor_of


def gaussian(stream_key, dims, scale, reach, cuts=(), kind=jnp.bfloat16):
    drawn = jax.random.normal(stream_key, dims, jnp.float32) * scale
    if len(cuts) > 0:
        drawn = shard_levels(stream_key, dims, cuts, -0.22, 0.18) * drawn
    return jnp.clip(drawn, min=-reach, max=reach).astype(kind)


def setup_inputs(seed: int = 0) -> dict:
    streams_of = jax.random.split(jax.random.key(seed), 6)
    intensity = gaussian(streams_of[0], (FRAMES, PIX), 1.0, 6.0, ((0, 4), (1, 8)))
    chi_bin = plant(jax.random.randint(streams_of[1], (PIX,), 0, NCHI), jax.random.fold_in(streams_of[1], 1), 0, NCHI - 1).astype(jnp.int32)
    split = jnp.clip(1.0 * jax.random.uniform(streams_of[2], (PIX,), jnp.float32) ** shard_levels(streams_of[2], (PIX,), ((0, 8),), -0.2, 0.2), 0.0, 1.0)
    mask = plant((jax.random.randint(streams_of[3], (PIX,), 0, 8) < 7).astype(jnp.int32), jax.random.fold_in(streams_of[3], 1), 0, 1)
    tile_row = draw_tile_row(jax.random.fold_in(streams_of[5], 71), 0)
    return dict(intensity=intensity, chi_bin=chi_bin, split=split, mask=mask, tile_row=tile_row)


def fourier_table():
    harmonic = lax.iota(jnp.int32, NH)[:, None]
    column = lax.iota(jnp.int32, NCHI)[None, :]
    phases = (harmonic * column % NCHI).astype(jnp.float32) * (2.0 * math.pi / NCHI)
    factor = 1.0 / math.sqrt(NCHI)
    return jnp.stack([jnp.cos(phases) * factor, -jnp.sin(phases) * factor], 0)

def reference(intensity, chi_bin, split, mask, tile_row):
    usable = mask.astype(jnp.float32)
    near_weight = lax.optimization_barrier((usable * split).astype(jnp.bfloat16)).astype(jnp.float32)
    far_weight = lax.optimization_barrier((usable * (1.0 - split)).astype(jnp.bfloat16)).astype(jnp.float32)
    tile_rows = jnp.repeat(tile_row, 128).astype(jnp.int32)
    near_bins = (tile_rows * NCHI + chi_bin).astype(jnp.int32)
    far_bins = (tile_rows * NCHI + (chi_bin + 1) % NCHI).astype(jnp.int32)
    bins_total = NQ * NCHI
    counts = jax.ops.segment_sum(near_weight, near_bins, bins_total) + jax.ops.segment_sum(far_weight, far_bins, bins_total)

    def bin_frame(frame):
        values = frame.astype(jnp.float32)
        return jax.ops.segment_sum(values * near_weight, near_bins, bins_total) + jax.ops.segment_sum(values * far_weight, far_bins, bins_total)
    sums = lax.map(bin_frame, intensity)
    normed = (sums / jnp.maximum(counts, 1.0)).reshape(FRAMES, NQ, NCHI)
    spectra = jnp.einsum('fqc,rnc->frnq', normed, fourier_table(), precision=lax.Precision.HIGHEST)
    real_part = spectra[:, 0]
    imag_part = spectra[:, 1]
    high = lax.Precision.HIGHEST
    real_corr = jnp.einsum('fnq,fnp->qnp', real_part, real_part, precision=high) + jnp.einsum('fnq,fnp->qnp', imag_part, imag_part, precision=high)
    imag_corr = jnp.einsum('fnq,fnp->qnp', imag_part, real_part, precision=high) - jnp.einsum('fnq,fnp->qnp', real_part, imag_part, precision=high)
    return jnp.stack([real_corr, imag_corr], 1) / math.sqrt(FRAMES)
```

```python
import functools
import math

import jax
import jax.numpy as jnp
from jax import lax
from jax.experimental import pallas as pl
from jax.experimental.pallas import tpu as pltpu
from jax.sharding import PartitionSpec as P

NQ = 256
NCHI = 256
NH = 128
LANES = 128
BF = jnp.bfloat16
F32 = jnp.float32
PIECES = 4
NT = (((1,), (1,)), ((), ()))
TN = (((0,), (0,)), ((), ()))


def pixel_weights(split, mask):
    usable = mask.astype(F32)
    near = (usable * split).astype(BF).astype(F32)
    far = (usable * (1.0 - split)).astype(BF).astype(F32)
    return near, far


def row_of(block, j, height):
    return jnp.broadcast_to(block[j : j + 1, :], (height, LANES)).astype(BF)


def tall(tile, times):
    return jnp.concatenate([tile] * times, 0)


def iota_rows(rows):
    return lax.broadcasted_iota(jnp.int32, (rows, LANES), 0).astype(F32).astype(BF)


def counts_kernel(rows, chi, split, mask, out, acc, *, tiles, unroll):
    acc[...] = jnp.zeros_like(acc)
    digits = iota_rows(16)
    zero = jnp.zeros((16, LANES), BF)
    one = jnp.ones((16, LANES), BF)

    def step(k, _):
        block = pl.ds(k * unroll, unroll)
        first = chi[block, :]
        second = (first + 1) & (NCHI - 1)
        near, far = pixel_weights(split[block, :], mask[block, :])
        high, low = (first >> 4).astype(F32), (first & 15).astype(F32)
        high2, low2 = (second >> 4).astype(F32), (second & 15).astype(F32)
        for j in range(unroll):
            row = lambda a: row_of(a, j, 16)
            left = jnp.concatenate(
                [jnp.where(digits == row(high), row(near), zero), jnp.where(digits == row(high2), row(far), zero)], 1
            )
            right = jnp.concatenate(
                [jnp.where(digits == row(low), one, zero), jnp.where(digits == row(low2), one, zero)], 1
            )
            total = lax.dot_general(left, right, NT, preferred_element_type=F32)
            q = rows[k * unroll + j]
            acc[q, :, 0:16] = acc[q, :, 0:16] + total
        return 0

    lax.fori_loop(0, tiles // unroll, step, 0)
    for h in range(16):
        out[:, 16 * h : 16 * h + 16] = acc[:, h, 0:16]


def bin_counts(rows, chi, split, mask):
    tiles = chi.shape[0]
    unroll = math.gcd(tiles, 8)
    whole = pl.BlockSpec((tiles, LANES), lambda i, r: (0, 0))
    return pl.pallas_call(
        functools.partial(counts_kernel, tiles=tiles, unroll=unroll),
        out_shape=jax.ShapeDtypeStruct((NQ, NCHI), F32),
        grid_spec=pltpu.PrefetchScalarGridSpec(
            num_scalar_prefetch=1,
            grid=(1,),
            in_specs=[whole] * 3,
            out_specs=pl.BlockSpec((NQ, NCHI), lambda i, r: (0, 0)),
            scratch_shapes=[pltpu.VMEM((NQ, 16, LANES), F32)],
        ),
        name="bin_counts",
    )(rows, chi, split, mask)


def cake_kernel(rows, pixels, chi, split, mask, out, *, block_tiles, unroll):
    grid_step = pl.program_id(0)

    @pl.when(grid_step == 0)
    def _():
        out[...] = jnp.zeros_like(out)

    columns = iota_rows(NCHI)
    zero = jnp.zeros((NCHI, LANES), BF)

    def step(k, _):
        block = pl.ds(k * unroll, unroll)
        first = chi[block, :]
        near, far = pixel_weights(split[block, :], mask[block, :])
        here = first.astype(F32)
        then = ((first + 1) & (NCHI - 1)).astype(F32)
        for j in range(unroll):
            row = lambda a: tall(row_of(a, j, 16), NCHI // 16)
            weights = jnp.where(columns == row(here), row(near), jnp.where(columns == row(then), row(far), zero))
            start = pl.multiple_of((k * unroll + j) * LANES, LANES)
            part = lax.dot_general(pixels[:, pl.ds(start, LANES)], weights, NT, preferred_element_type=F32)
            q = rows[grid_step * block_tiles + k * unroll + j]
            out[q] = out[q] + part
        return 0

    lax.fori_loop(0, block_tiles // unroll, step, 0)


def bin_cake(rows, pixels, chi, split, mask):
    frames, tiles = pixels.shape[0], chi.shape[0]
    block_tiles = math.gcd(tiles, 64)
    unroll = math.gcd(block_tiles, 8)
    small = pl.BlockSpec((block_tiles, LANES), lambda i, r: (i, 0))
    return pl.pallas_call(
        functools.partial(cake_kernel, block_tiles=block_tiles, unroll=unroll),
        out_shape=jax.ShapeDtypeStruct((NQ, frames, NCHI), F32),
        grid_spec=pltpu.PrefetchScalarGridSpec(
            num_scalar_prefetch=1,
            grid=(tiles // block_tiles,),
            in_specs=[pl.BlockSpec((frames, block_tiles * LANES), lambda i, r: (0, i)), small, small, small],
            out_specs=pl.BlockSpec((NQ, frames, NCHI), lambda i, r: (0, 0, 0)),
        ),
        name="bin_cake",
    )(rows, pixels, chi, split, mask)


def halves(x):
    high = x.astype(BF)
    return high, (x - high.astype(F32)).astype(BF)


def spectra_kernel(cake, counts, table, *rest, block_frames):
    outs, inverse = rest[:-1], rest[-1]

    @pl.when(pl.program_id(0) == 0)
    def _():
        inverse[...] = 1.0 / jnp.maximum(counts[...], 1.0)

    t_high, t_low = table[0], table[1]
    for f in range(block_frames):
        x_high, x_low = halves(cake[:, f, :] * inverse[...])
        dot = lambda a, b: lax.dot_general(a, b, NT, preferred_element_type=F32)
        spectrum = dot(t_high, x_high) + (dot(t_high, x_low) + dot(t_low, x_high))
        first = 0
        for out in outs:
            out[:, f, :] = spectrum[first : first + out.shape[0], :]
            first += out.shape[0]


def chi_spectra(cake, counts, table, parts):
    frames = cake.shape[1]
    block_frames = 8
    rows = table.shape[1] // parts
    return pl.pallas_call(
        functools.partial(spectra_kernel, block_frames=block_frames),
        out_shape=[jax.ShapeDtypeStruct((rows, frames, NQ), F32)] * parts,
        grid_spec=pltpu.PrefetchScalarGridSpec(
            num_scalar_prefetch=0,
            grid=(frames // block_frames,),
            in_specs=[
                pl.BlockSpec((NQ, block_frames, NCHI), lambda i: (0, i, 0)),
                pl.BlockSpec((NQ, NCHI), lambda i: (0, 0)),
                pl.BlockSpec(table.shape, lambda i: (0, 0, 0)),
            ],
            out_specs=[pl.BlockSpec((rows, block_frames, NQ), lambda i: (0, i, 0))] * parts,
            scratch_shapes=[pltpu.VMEM((NQ, NCHI), F32)],
        ),
        name="chi_spectra",
    )(cake, counts, table)


def correlation_kernel(place, *refs, groups, harmonics, q_block, scale):
    out = refs[-1]
    offset = place[0] * q_block
    base = pl.multiple_of((offset // LANES) * LANES, LANES)
    offset = offset % LANES
    lane = lax.broadcasted_iota(jnp.int32, (1, LANES), 1)
    per = len(refs[:-1]) // groups
    for group in range(groups):
        members = refs[group * per : group * per + per]
        for n in range(harmonics):
            real = jnp.concatenate([m[0, n] for m in members], 0)
            imag = jnp.concatenate([m[1, n] for m in members], 0)
            right = jnp.concatenate([real, imag], 0)
            own_a = jnp.concatenate([m[0, n, :, pl.ds(base, LANES)] for m in members], 0)
            own_b = jnp.concatenate([m[1, n, :, pl.ds(base, LANES)] for m in members], 0)
            z = jnp.concatenate([own_a, own_b], 0)
            y = jnp.concatenate([own_b, -own_a], 0)
            z = pltpu.roll(z, (LANES - offset) % LANES, 1)
            y = pltpu.roll(y, (LANES + q_block - offset) % LANES, 1)
            left = jnp.where(lane < q_block, z, y)
            l_high, l_low = halves(left * scale)
            r_high, r_low = halves(right)
            dot = lambda a, b: lax.dot_general(a, b, TN, preferred_element_type=F32)
            result = dot(l_high, r_high) + (dot(l_high, r_low) + dot(l_low, r_high))
            where = group * harmonics + n
            out[:, 0, where, :] = result[:q_block]
            out[:, 1, where, :] = result[q_block : 2 * q_block]


def correlate(place, pieces, q_block, scale):
    harmonics = pieces[0][0].shape[1]
    flat = [m for members in pieces for m in members]
    full = pl.BlockSpec(flat[0].shape, lambda i, r: (0, 0, 0, 0))
    total = harmonics * len(pieces)
    shape = (q_block, 2, total, NQ)
    return pl.pallas_call(
        functools.partial(
            correlation_kernel, groups=len(pieces), harmonics=harmonics, q_block=q_block, scale=scale
        ),
        out_shape=jax.ShapeDtypeStruct(shape, F32),
        grid_spec=pltpu.PrefetchScalarGridSpec(
            num_scalar_prefetch=1,
            grid=(1,),
            in_specs=[full] * len(flat),
            out_specs=pl.BlockSpec(shape, lambda i, r: (0, 0, 0, 0)),
        ),
        name="correlate",
    )(place, *flat)


def make_body(mesh):
    frame_ranks, pix_ranks = mesh.shape["frames"], mesh.shape["pix"]
    stages = pix_ranks // 2
    owned = NH // pix_ranks
    pieces = PIECES if owned % PIECES == 0 else 1
    per_piece = owned // pieces
    q_block = NQ // frame_ranks
    partner = [(i, i ^ 1) for i in range(pix_ranks)]
    ring = [(i, (i + 2) % pix_ranks) for i in range(pix_ranks)]

    def fourier_table(pix):
        stage, core = pix // 2, pix % 2
        shape = (pieces, 2, stages, 2, per_piece, NCHI)
        axis = lambda d: lax.broadcasted_iota(jnp.int32, shape, d)
        owner_stage = (stage - 1 - axis(2)) % stages
        owner_core = jnp.where(axis(1) == 0, 1 - core, core)
        harmonic = (owner_stage * 2 + owner_core) * owned + axis(0) * per_piece + axis(4)
        phase = (harmonic * axis(5) % NCHI).astype(F32) * (2.0 * math.pi / NCHI)
        factor = 1.0 / math.sqrt(NCHI)
        table = jnp.where(axis(3) == 0, jnp.cos(phase), -jnp.sin(phase)) * factor
        table = table.reshape(2 * NH, NCHI)
        high = lax.reduce_precision(table, 8, 7)
        return jnp.stack([high, table - high]).astype(BF)

    def sum_counts(counts, pix):
        core = pix % 2
        pair = counts.reshape(2, NQ // 2, NCHI)
        mine = lax.dynamic_index_in_dim(pair, core, 0, False)
        other = lax.dynamic_index_in_dim(pair, 1 - core, 0, False)
        mine = mine + lax.ppermute(other, "pix", partner)
        total = mine
        for hop in range(1, stages):
            shift = [(i, (i + 2 * hop) % pix_ranks) for i in range(pix_ranks)]
            total = total + lax.ppermute(mine, "pix", shift)
        other = lax.ppermute(total, "pix", partner)
        first = jnp.where(core == 0, total, other)
        second = jnp.where(core == 0, other, total)
        return jnp.concatenate([first, second], 0)

    def gather_frames(x):
        members = [x]
        for hop in range(1, frame_ranks):
            members.append(lax.ppermute(x, "frames", [(i, i ^ hop) for i in range(frame_ranks)]))
        return members

    def body(intensity, chi_bin, split, mask, tile_row):
        frames_dev = intensity.shape[0]
        frames = frames_dev * frame_ranks
        pix = lax.axis_index("pix")
        flat = lambda a: a.reshape(-1, LANES)
        pixel_args = (flat(chi_bin), flat(split), flat(mask))
        counts = sum_counts(bin_counts(tile_row, *pixel_args), pix)
        cake = bin_cake(tile_row, intensity, *pixel_args)
        parts = chi_spectra(cake, counts, fourier_table(pix), 2 * pieces)
        shape = (stages, 2, per_piece, frames_dev, NQ)
        gathered = []
        for piece in range(pieces):
            send = parts[2 * piece].reshape(shape)
            keep = parts[2 * piece + 1].reshape(shape)
            both = lax.ppermute(send, "pix", partner)
            partial_sum = keep[0] + both[0]
            for stage in range(1, stages):
                partial_sum = lax.ppermute(partial_sum, "pix", ring)
                partial_sum = partial_sum + (keep[stage] + both[stage])
            gathered.append(gather_frames(partial_sum))
        place = lax.axis_index("frames").astype(jnp.int32).reshape(1)
        per_call = max(1, 8 // per_piece)
        outs = [
            correlate(place, gathered[i : i + per_call], q_block, 1.0 / math.sqrt(frames))
            for i in range(0, pieces, per_call)
        ]
        return jnp.concatenate(outs, 2)

    return body


def solution(mesh):
    in_specs = (P("frames", "pix"), P("pix"), P("pix"), P("pix"), P("pix"))
    out_specs = P("frames", None, "pix", None)
    return jax.shard_map(make_body(mesh), mesh=mesh, in_specs=in_specs, out_specs=out_specs, check_vma=False)
```

```python
import functools
import math

import jax
import jax.numpy as jnp
from jax import lax
from jax.experimental import pallas as pl
from jax.experimental.pallas import tpu as pltpu
from jax.sharding import PartitionSpec as P


NQ = 256
NCHI = 256
NH = 128
LANES = 128
BF = jnp.bfloat16
F32 = jnp.float32
GROUP = 8
NT = (((1,), (1,)), ((), ()))
TN = (((0,), (0,)), ((), ()))


def pixel_weights(split, mask):
    usable = mask.astype(F32)
    near = (usable * split).astype(BF).astype(F32)
    far = (usable * (1.0 - split)).astype(BF).astype(F32)
    return near, far


def row_of(block, j, height):
    return jnp.broadcast_to(block[j : j + 1, :], (height, LANES)).astype(BF)


def tall(tile, times):
    return jnp.concatenate([tile] * times, 0)


def iota_rows(rows):
    return lax.broadcasted_iota(jnp.int32, (rows, LANES), 0).astype(F32).astype(BF)


def counts_kernel(rows, chi, split, mask, out, acc, *, tiles, unroll):
    acc[...] = jnp.zeros_like(acc)
    digits = iota_rows(16)
    zero = jnp.zeros((16, LANES), BF)
    one = jnp.ones((16, LANES), BF)

    def step(k, _):
        block = pl.ds(k * unroll, unroll)
        first = chi[block, :]
        second = (first + 1) & (NCHI - 1)
        near, far = pixel_weights(split[block, :], mask[block, :])
        high, low = (first >> 4).astype(F32), (first & 15).astype(F32)
        high2, low2 = (second >> 4).astype(F32), (second & 15).astype(F32)
        for j in range(unroll):
            row = lambda a: row_of(a, j, 16)
            left = jnp.concatenate(
                [jnp.where(digits == row(high), row(near), zero), jnp.where(digits == row(high2), row(far), zero)], 1
            )
            right = jnp.concatenate(
                [jnp.where(digits == row(low), one, zero), jnp.where(digits == row(low2), one, zero)], 1
            )
            total = lax.dot_general(left, right, NT, preferred_element_type=F32)
            q = rows[k * unroll + j]
            acc[q, :, 0:16] = acc[q, :, 0:16] + total
        return 0

    lax.fori_loop(0, tiles // unroll, step, 0)
    for h in range(16):
        out[:, 16 * h : 16 * h + 16] = acc[:, h, 0:16]


def bin_counts(rows, chi, split, mask):
    tiles = chi.shape[0]
    unroll = math.gcd(tiles, 64)
    whole = pl.BlockSpec((tiles, LANES), lambda i, r: (0, 0))
    return pl.pallas_call(
        functools.partial(counts_kernel, tiles=tiles, unroll=unroll),
        out_shape=jax.ShapeDtypeStruct((NQ, NCHI), F32),
        grid_spec=pltpu.PrefetchScalarGridSpec(
            num_scalar_prefetch=1,
            grid=(1,),
            in_specs=[whole] * 3,
            out_specs=pl.BlockSpec((NQ, NCHI), lambda i, r: (0, 0)),
            scratch_shapes=[pltpu.VMEM((NQ, 16, LANES), F32)],
        ),
        name="bin_counts",
    )(rows, chi, split, mask)


def cake_kernel(rows, pixels, chi, split, mask, out, *, block_tiles, unroll):
    grid_step = pl.program_id(0)

    @pl.when(grid_step == 0)
    def _():
        out[...] = jnp.zeros_like(out)

    columns = iota_rows(NCHI)
    zero = jnp.zeros((NCHI, LANES), BF)

    def step(k, _):
        block = pl.ds(k * unroll, unroll)
        first = chi[block, :]
        near, far = pixel_weights(split[block, :], mask[block, :])
        here = first.astype(F32)
        then = ((first + 1) & (NCHI - 1)).astype(F32)
        for j in range(unroll):
            row = lambda a: tall(row_of(a, j, 16), NCHI // 16)
            weights = jnp.where(columns == row(here), row(near), jnp.where(columns == row(then), row(far), zero))
            start = pl.multiple_of((k * unroll + j) * LANES, LANES)
            part = lax.dot_general(pixels[:, pl.ds(start, LANES)], weights, NT, preferred_element_type=F32)
            q = rows[grid_step * block_tiles + k * unroll + j]
            out[q] = out[q] + part
        return 0

    lax.fori_loop(0, block_tiles // unroll, step, 0)


def bin_cake(rows, pixels, chi, split, mask):
    frames, tiles = pixels.shape[0], chi.shape[0]
    block_tiles = math.gcd(tiles, 64)
    unroll = math.gcd(block_tiles, 32)
    small = pl.BlockSpec((block_tiles, LANES), lambda i, r: (i, 0))
    return pl.pallas_call(
        functools.partial(cake_kernel, block_tiles=block_tiles, unroll=unroll),
        out_shape=jax.ShapeDtypeStruct((NQ, frames, NCHI), F32),
        grid_spec=pltpu.PrefetchScalarGridSpec(
            num_scalar_prefetch=1,
            grid=(tiles // block_tiles,),
            in_specs=[pl.BlockSpec((frames, block_tiles * LANES), lambda i, r: (0, i)), small, small, small],
            out_specs=pl.BlockSpec((NQ, frames, NCHI), lambda i, r: (0, 0, 0)),
        ),
        cost_estimate=pl.CostEstimate(
            flops=32 * frames * NCHI * tiles * LANES, transcendentals=0, bytes_accessed=64 * frames * tiles * LANES
        ),
        name="bin_cake",
    )(rows, pixels, chi, split, mask)


def halves(x):
    high = x.astype(BF)
    return high, (x - high.astype(F32)).astype(BF)


def spectra_kernel(cake, counts, table, *outs):
    inverse = 1.0 / jnp.maximum(counts[...], 1.0)
    t_high, t_low = table[0], table[1]
    for f in range(GROUP):
        x_high, x_low = halves(cake[:, f, :] * inverse)
        dot = lambda a, b: lax.dot_general(a, b, NT, preferred_element_type=F32)
        spectrum = dot(t_high, x_high) + (dot(t_high, x_low) + dot(t_low, x_high))
        first = 0
        for out in outs:
            out[:, f, :] = spectrum[first : first + out.shape[0], :]
            first += out.shape[0]


def chi_spectra(cake, counts, table, piece, parts):
    rows = table.shape[1] // parts
    return pl.pallas_call(
        spectra_kernel,
        out_shape=[jax.ShapeDtypeStruct((rows, GROUP, NQ), F32)] * parts,
        grid_spec=pltpu.PrefetchScalarGridSpec(
            num_scalar_prefetch=0,
            grid=(NQ // LANES,),
            in_specs=[
                pl.BlockSpec((LANES, GROUP, NCHI), lambda i: (i, piece, 0)),
                pl.BlockSpec((LANES, NCHI), lambda i: (i, 0)),
                pl.BlockSpec(table.shape, lambda i: (0, 0, 0)),
            ],
            out_specs=[pl.BlockSpec((rows, GROUP, LANES), lambda i: (0, 0, i))] * parts,
        ),
        name="chi_spectra",
    )(cake, counts, table)


def correlation_kernel(place, *refs, harmonics, q_block, scale, members, add):
    out = refs[-1]
    before = refs[members] if add else None
    refs = refs[:members]
    offset = place[0] * q_block
    base = pl.multiple_of((offset // LANES) * LANES, LANES)
    offset = offset % LANES
    lane = lax.broadcasted_iota(jnp.int32, (1, LANES), 1)
    for n in range(harmonics):
        real = jnp.concatenate([m[0, n] for m in refs], 0)
        imag = jnp.concatenate([m[1, n] for m in refs], 0)
        right = jnp.concatenate([real, imag], 0)
        own_a = jnp.concatenate([m[0, n, :, pl.ds(base, LANES)] for m in refs], 0)
        own_b = jnp.concatenate([m[1, n, :, pl.ds(base, LANES)] for m in refs], 0)
        z = jnp.concatenate([own_a, own_b], 0)
        y = jnp.concatenate([own_b, -own_a], 0)
        z = pltpu.roll(z, (LANES - offset) % LANES, 1)
        y = pltpu.roll(y, (LANES + q_block - offset) % LANES, 1)
        left = jnp.where(lane < q_block, z, y)
        l_high, l_low = halves(left * scale)
        r_high, r_low = halves(right)
        dot = lambda a, b: lax.dot_general(a, b, TN, preferred_element_type=F32)
        result = dot(l_high, r_high) + (dot(l_high, r_low) + dot(l_low, r_high))
        for part in range(2):
            value = result[part * q_block : (part + 1) * q_block]
            if add:
                value = value + before[:, part, n, :]
            out[:, part, n, :] = value


def correlate(place, members, q_block, scale, before):
    owned = members[0].shape[1]
    harmonics = math.gcd(owned, 8)
    block = (2, harmonics) + members[0].shape[2:]
    out_spec = pl.BlockSpec((q_block, 2, harmonics, NQ), lambda i, r: (0, 0, i, 0))
    extra = [] if before is None else [before]
    return pl.pallas_call(
        functools.partial(
            correlation_kernel,
            harmonics=harmonics,
            q_block=q_block,
            scale=scale,
            members=len(members),
            add=before is not None,
        ),
        out_shape=jax.ShapeDtypeStruct((q_block, 2, owned, NQ), F32),
        grid_spec=pltpu.PrefetchScalarGridSpec(
            num_scalar_prefetch=1,
            grid=(owned // harmonics,),
            in_specs=[pl.BlockSpec(block, lambda i, r: (0, i, 0, 0))] * len(members) + [out_spec] * len(extra),
            out_specs=out_spec,
        ),
        input_output_aliases={1 + len(members): 0} if extra else {},
        name="correlate",
    )(place, *members, *extra)


def ring_order(pieces, steps):
    done, latest, order = [0] * pieces, [-2] * pieces, []
    for slot in range(2 * pieces * steps + 2):
        ready = [p for p in range(pieces) if done[p] < steps and latest[p] <= slot - 2]
        if ready:
            order.append((ready[0], done[ready[0]] + 1))
            done[ready[0]] += 1
            latest[ready[0]] = slot
    return order


def make_body(mesh):
    frame_ranks, pix_ranks = mesh.shape["frames"], mesh.shape["pix"]
    stages = pix_ranks // 2
    owned = NH // pix_ranks
    q_block = NQ // frame_ranks
    partner = [(i, i ^ 1) for i in range(pix_ranks)]
    ring = [(i, (i + 2) % pix_ranks) for i in range(pix_ranks)]

    def fourier_table(pix):
        stage, core = pix // 2, pix % 2
        shape = (2, stages, 2, owned, NCHI)
        axis = lambda d: lax.broadcasted_iota(jnp.int32, shape, d)
        owner_stage = (stage - 1 - axis(1)) % stages
        owner_core = jnp.where(axis(0) == 0, 1 - core, core)
        harmonic = (owner_stage * 2 + owner_core) * owned + axis(3)
        phase = (harmonic * axis(4) % NCHI).astype(F32) * (2.0 * math.pi / NCHI)
        factor = 1.0 / math.sqrt(NCHI)
        table = jnp.where(axis(2) == 0, jnp.cos(phase), -jnp.sin(phase)) * factor
        table = table.reshape(2 * NH, NCHI)
        high = lax.reduce_precision(table, 8, 7)
        return jnp.stack([high, table - high]).astype(BF)

    def sum_counts(counts, pix):
        core = pix % 2
        pair = counts.reshape(2, NQ // 2, NCHI)
        mine = lax.dynamic_index_in_dim(pair, core, 0, False)
        other = lax.dynamic_index_in_dim(pair, 1 - core, 0, False)
        mine = mine + lax.ppermute(other, "pix", partner)
        total = mine
        for hop in range(1, stages):
            shift = [(i, (i + 2 * hop) % pix_ranks) for i in range(pix_ranks)]
            total = total + lax.ppermute(mine, "pix", shift)
        other = lax.ppermute(total, "pix", partner)
        first = jnp.where(core == 0, total, other)
        second = jnp.where(core == 0, other, total)
        return jnp.concatenate([first, second], 0)

    def gather_frames(x):
        members = [x]
        for hop in range(1, frame_ranks):
            pairs = [(i, i ^ hop) for i in range(frame_ranks)]
            members.append(lax.ppermute(x, "frames", pairs))
        return members

    def body(intensity, chi_bin, split, mask, tile_row):
        frames_dev = intensity.shape[0]
        frames = frames_dev * frame_ranks
        pix = lax.axis_index("pix")
        flat = lambda a: a.reshape(-1, LANES)
        pixel_args = (flat(chi_bin), flat(split), flat(mask))
        counts = sum_counts(bin_counts(tile_row, *pixel_args), pix)
        cake = bin_cake(tile_row, intensity, *pixel_args)
        table = fourier_table(pix)
        pieces = frames_dev // GROUP
        shape = (stages, 2, owned, GROUP, NQ)
        sums, keeps, boths = [None] * pieces, [None] * pieces, [None] * pieces
        for piece in range(pieces):
            send, keep = chi_spectra(cake, counts, table, piece, 2)
            keeps[piece] = keep.reshape(shape)
            boths[piece] = lax.ppermute(send.reshape(shape), "pix", partner)
            sums[piece] = keeps[piece][0] + boths[piece][0]
        for piece, stage in ring_order(pieces, stages - 1):
            received = lax.ppermute(sums[piece], "pix", ring)
            sums[piece] = received + (keeps[piece][stage] + boths[piece][stage])
        gathered = [gather_frames(s) for s in sums]
        place = lax.axis_index("frames").astype(jnp.int32).reshape(1)
        scale = 1.0 / math.sqrt(frames)
        out = None
        for group in (gathered[:-1], gathered[-1:]):
            if group:
                out = correlate(place, [m for members in group for m in members], q_block, scale, out)
        return out

    return body


def solution(mesh):
    in_specs = (P("frames", "pix"), P("pix"), P("pix"), P("pix"), P("pix"))
    out_specs = P("frames", None, "pix", None)
    body = make_body(mesh)

    return jax.shard_map(body, mesh=mesh, in_specs=in_specs, out_specs=out_specs, check_vma=False)
```

```python
import functools
import math

import jax
import jax.numpy as jnp
from jax import lax
from jax.experimental import pallas as pl
from jax.experimental.pallas import tpu as pltpu
from jax.sharding import PartitionSpec as P


NQ = 256
NCHI = 256
NH = 128
LANES = 128
BF = jnp.bfloat16
F32 = jnp.float32
GROUP = 8
NT = (((1,), (1,)), ((), ()))
TN = (((0,), (0,)), ((), ()))


def pixel_weights(split, mask):
    usable = mask.astype(F32)
    near = (usable * split).astype(BF).astype(F32)
    far = (usable * (1.0 - split)).astype(BF).astype(F32)
    return near, far


def row_of(block, j, height):
    return jnp.broadcast_to(block[j : j + 1, :], (height, LANES)).astype(BF)


def tall(tile, times):
    return jnp.concatenate([tile] * times, 0)


def iota_rows(rows):
    return lax.broadcasted_iota(jnp.int32, (rows, LANES), 0).astype(F32).astype(BF)


def counts_kernel(rows, chi, split, mask, out, acc, *, tiles, unroll):
    acc[...] = jnp.zeros_like(acc)
    digits = iota_rows(16)
    zero = jnp.zeros((16, LANES), BF)
    one = jnp.ones((16, LANES), BF)

    def step(k, _):
        block = pl.ds(k * unroll, unroll)
        first = chi[block, :]
        second = (first + 1) & (NCHI - 1)
        near, far = pixel_weights(split[block, :], mask[block, :])
        high, low = (first >> 4).astype(F32), (first & 15).astype(F32)
        high2, low2 = (second >> 4).astype(F32), (second & 15).astype(F32)
        for j in range(unroll):
            row = lambda a: row_of(a, j, 16)
            left = jnp.concatenate(
                [jnp.where(digits == row(high), row(near), zero), jnp.where(digits == row(high2), row(far), zero)], 1
            )
            right = jnp.concatenate(
                [jnp.where(digits == row(low), one, zero), jnp.where(digits == row(low2), one, zero)], 1
            )
            total = lax.dot_general(left, right, NT, preferred_element_type=F32)
            q = rows[k * unroll + j]
            acc[q, :, 0:16] = acc[q, :, 0:16] + total
        return 0

    lax.fori_loop(0, tiles // unroll, step, 0)
    for h in range(16):
        out[:, 16 * h : 16 * h + 16] = acc[:, h, 0:16]


def bin_counts(rows, chi, split, mask):
    tiles = chi.shape[0]
    unroll = math.gcd(tiles, 64)
    whole = pl.BlockSpec((tiles, LANES), lambda i, r: (0, 0))
    return pl.pallas_call(
        functools.partial(counts_kernel, tiles=tiles, unroll=unroll),
        out_shape=jax.ShapeDtypeStruct((NQ, NCHI), F32),
        grid_spec=pltpu.PrefetchScalarGridSpec(
            num_scalar_prefetch=1,
            grid=(1,),
            in_specs=[whole] * 3,
            out_specs=pl.BlockSpec((NQ, NCHI), lambda i, r: (0, 0)),
            scratch_shapes=[pltpu.VMEM((NQ, 16, LANES), F32)],
        ),
        name="bin_counts",
    )(rows, chi, split, mask)


def cake_kernel(rows, pixels, chi, split, mask, out, *, block_tiles, unroll):
    grid_step = pl.program_id(0)

    @pl.when(grid_step == 0)
    def _():
        out[...] = jnp.zeros_like(out)

    columns = iota_rows(NCHI)
    zero = jnp.zeros((NCHI, LANES), BF)

    def step(k, _):
        block = pl.ds(k * unroll, unroll)
        first = chi[block, :]
        near, far = pixel_weights(split[block, :], mask[block, :])
        here = first.astype(F32)
        then = ((first + 1) & (NCHI - 1)).astype(F32)
        for j in range(unroll):
            row = lambda a: tall(row_of(a, j, 16), NCHI // 16)
            weights = jnp.where(columns == row(here), row(near), jnp.where(columns == row(then), row(far), zero))
            start = pl.multiple_of((k * unroll + j) * LANES, LANES)
            part = lax.dot_general(pixels[:, pl.ds(start, LANES)], weights, NT, preferred_element_type=F32)
            q = rows[grid_step * block_tiles + k * unroll + j]
            out[q] = out[q] + part
        return 0

    lax.fori_loop(0, block_tiles // unroll, step, 0)


def bin_cake(rows, pixels, chi, split, mask):
    frames, tiles = pixels.shape[0], chi.shape[0]
    block_tiles = math.gcd(tiles, 64)
    unroll = math.gcd(block_tiles, 64)
    small = pl.BlockSpec((block_tiles, LANES), lambda i, r: (i, 0))
    return pl.pallas_call(
        functools.partial(cake_kernel, block_tiles=block_tiles, unroll=unroll),
        out_shape=jax.ShapeDtypeStruct((NQ, frames, NCHI), F32),
        grid_spec=pltpu.PrefetchScalarGridSpec(
            num_scalar_prefetch=1,
            grid=(tiles // block_tiles,),
            in_specs=[pl.BlockSpec((frames, block_tiles * LANES), lambda i, r: (0, i)), small, small, small],
            out_specs=pl.BlockSpec((NQ, frames, NCHI), lambda i, r: (0, 0, 0)),
        ),
        cost_estimate=pl.CostEstimate(
            flops=32 * frames * NCHI * tiles * LANES, transcendentals=0, bytes_accessed=64 * frames * tiles * LANES
        ),
        name="bin_cake",
    )(rows, pixels, chi, split, mask)


def halves(x):
    high = x.astype(BF)
    return high, (x - high.astype(F32)).astype(BF)


def spectra_kernel(cake, counts, table, *outs, parts, blocks):
    inverse = 1.0 / jnp.maximum(counts[...], 1.0)
    factors = jnp.concatenate([table[0], table[0], table[1]], 1)
    piece = pl.program_id(0) // blocks
    for own in range(len(outs) // parts):

        @pl.when(piece == own)
        def _():
            for f in range(GROUP):
                x_high, x_low = halves(cake[:, f, :] * inverse)
                values = jnp.concatenate([x_high, x_low, x_high], 1)
                spectrum = lax.dot_general(factors, values, NT, preferred_element_type=F32)
                first = 0
                for out in outs[own * parts : (own + 1) * parts]:
                    out[:, f, :] = spectrum[first : first + out.shape[0], :]
                    first += out.shape[0]


def chi_spectra(cake, counts, table, first, pieces, parts):
    rows = table.shape[1] // parts
    blocks = NQ // LANES
    own_block = lambda own: lambda i: (0, 0, jnp.clip(i - own * blocks, 0, blocks - 1))
    return pl.pallas_call(
        functools.partial(spectra_kernel, parts=parts, blocks=blocks),
        out_shape=[jax.ShapeDtypeStruct((rows, GROUP, NQ), F32)] * (parts * pieces),
        grid_spec=pltpu.PrefetchScalarGridSpec(
            num_scalar_prefetch=0,
            grid=(blocks * pieces,),
            in_specs=[
                pl.BlockSpec((LANES, GROUP, NCHI), lambda i: (i % blocks, first + i // blocks, 0)),
                pl.BlockSpec((LANES, NCHI), lambda i: (i % blocks, 0)),
                pl.BlockSpec(table.shape, lambda i: (0, 0, 0)),
            ],
            out_specs=[
                pl.BlockSpec((rows, GROUP, LANES), own_block(own)) for own in range(pieces) for _ in range(parts)
            ],
        ),
        name="chi_spectra",
    )(cake, counts, table)


def correlation_kernel(place, *refs, harmonics, q_block, scale, members, add):
    out = refs[-1]
    before = refs[members] if add else None
    refs = refs[:members]
    offset = place[0] * q_block
    base = pl.multiple_of((offset // LANES) * LANES, LANES)
    offset = offset % LANES
    lane = lax.broadcasted_iota(jnp.int32, (1, LANES), 1)
    for n in range(harmonics):
        real = jnp.concatenate([m[0, n] for m in refs], 0)
        imag = jnp.concatenate([m[1, n] for m in refs], 0)
        right = jnp.concatenate([real, imag], 0)
        own_a = jnp.concatenate([m[0, n, :, pl.ds(base, LANES)] for m in refs], 0)
        own_b = jnp.concatenate([m[1, n, :, pl.ds(base, LANES)] for m in refs], 0)
        z = jnp.concatenate([own_a, own_b], 0)
        y = jnp.concatenate([own_b, -own_a], 0)
        z = pltpu.roll(z, (LANES - offset) % LANES, 1)
        y = pltpu.roll(y, (LANES + q_block - offset) % LANES, 1)
        left = jnp.where(lane < q_block, z, y)
        l_high, l_low = halves(left * scale)
        r_high, r_low = halves(right)
        left = jnp.concatenate([l_high, l_high, l_low], 0)
        right = jnp.concatenate([r_high, r_low, r_high], 0)
        result = lax.dot_general(left, right, TN, preferred_element_type=F32)
        for part in range(2):
            value = result[part * q_block : (part + 1) * q_block]
            if add:
                value = value + before[:, part, n, :]
            out[:, part, n, :] = value


def correlate(place, members, q_block, scale, before):
    owned = members[0].shape[1]
    harmonics = math.gcd(owned, 8)
    block = (2, harmonics) + members[0].shape[2:]
    out_spec = pl.BlockSpec((q_block, 2, harmonics, NQ), lambda i, r: (0, 0, i, 0))
    extra = [] if before is None else [before]
    return pl.pallas_call(
        functools.partial(
            correlation_kernel,
            harmonics=harmonics,
            q_block=q_block,
            scale=scale,
            members=len(members),
            add=before is not None,
        ),
        out_shape=jax.ShapeDtypeStruct((q_block, 2, owned, NQ), F32),
        grid_spec=pltpu.PrefetchScalarGridSpec(
            num_scalar_prefetch=1,
            grid=(owned // harmonics,),
            in_specs=[pl.BlockSpec(block, lambda i, r: (0, i, 0, 0))] * len(members) + [out_spec] * len(extra),
            out_specs=out_spec,
        ),
        input_output_aliases={1 + len(members): 0} if extra else {},
        name="correlate",
    )(place, *members, *extra)


def ring_order(pieces, steps):
    slots = []
    for piece in range(pieces):
        base = piece // 2 * (2 * steps - 1)
        for k in range(steps):
            slot = base + 2 * k
            if piece % 2 and piece + 1 == pieces:
                slot += 3
            elif piece % 2:
                slot = base + 2 * steps if k + 1 == steps else slot + 1
            slots.append((slot, piece, k + 1))
    return [step[1:] for step in sorted(slots)]


def make_body(mesh):
    frame_ranks, pix_ranks = mesh.shape["frames"], mesh.shape["pix"]
    stages = pix_ranks // 2
    owned = NH // pix_ranks
    q_block = NQ // frame_ranks
    partner = [(i, i ^ 1) for i in range(pix_ranks)]
    ring = [(i, (i + 2) % pix_ranks) for i in range(pix_ranks)]

    def fourier_table(pix):
        stage, core = pix // 2, pix % 2
        shape = (2, stages, 2, owned, NCHI)
        axis = lambda d: lax.broadcasted_iota(jnp.int32, shape, d)
        owner_stage = (stage - 1 - axis(1)) % stages
        owner_core = jnp.where(axis(0) == 0, 1 - core, core)
        harmonic = (owner_stage * 2 + owner_core) * owned + axis(3)
        phase = (harmonic * axis(4) % NCHI).astype(F32) * (2.0 * math.pi / NCHI)
        factor = 1.0 / math.sqrt(NCHI)
        table = jnp.where(axis(2) == 0, jnp.cos(phase), -jnp.sin(phase)) * factor
        table = table.reshape(2 * NH, NCHI)
        high = lax.reduce_precision(table, 8, 7)
        return jnp.stack([high, table - high]).astype(BF)

    def sum_counts(counts, pix):
        core = pix % 2
        pair = counts.reshape(2, NQ // 2, NCHI)
        mine = lax.dynamic_index_in_dim(pair, core, 0, False)
        other = lax.dynamic_index_in_dim(pair, 1 - core, 0, False)
        mine = mine + lax.ppermute(other, "pix", partner)
        total = mine
        for hop in range(1, stages):
            shift = [(i, (i + 2 * hop) % pix_ranks) for i in range(pix_ranks)]
            total = total + lax.ppermute(mine, "pix", shift)
        other = lax.ppermute(total, "pix", partner)
        first = jnp.where(core == 0, total, other)
        second = jnp.where(core == 0, other, total)
        return jnp.concatenate([first, second], 0)

    def gather_frames(x):
        members = [x]
        for hop in range(1, frame_ranks):
            pairs = [(i, i ^ hop) for i in range(frame_ranks)]
            members.append(lax.ppermute(x, "frames", pairs))
        return members

    def body(intensity, chi_bin, split, mask, tile_row):
        frames_dev = intensity.shape[0]
        frames = frames_dev * frame_ranks
        pix = lax.axis_index("pix")
        flat = lambda a: a.reshape(-1, LANES)
        pixel_args = (flat(chi_bin), flat(split), flat(mask))
        counts = sum_counts(bin_counts(tile_row, *pixel_args), pix)
        cake = bin_cake(tile_row, intensity, *pixel_args)
        table = fourier_table(pix)
        pieces = frames_dev // GROUP
        shape = (stages, 2, owned, GROUP, NQ)
        sums, keeps, boths = [None] * pieces, [None] * pieces, [None] * pieces
        made = []
        for first in range(0, pieces, 2):
            made += chi_spectra(cake, counts, table, first, min(2, pieces - first), 2)
        for piece in range(pieces):
            send, keep = made[2 * piece], made[2 * piece + 1]
            keeps[piece] = keep.reshape(shape)
            boths[piece] = lax.ppermute(send.reshape(shape), "pix", partner)
            sums[piece] = keeps[piece][0] + boths[piece][0]
        for piece, stage in ring_order(pieces, stages - 1):
            received = lax.ppermute(sums[piece], "pix", ring)
            sums[piece] = received + (keeps[piece][stage] + boths[piece][stage])
        gathered = [gather_frames(s) for s in sums]
        place = lax.axis_index("frames").astype(jnp.int32).reshape(1)
        scale = 1.0 / math.sqrt(frames)
        out = None
        for group in (gathered[:-1], gathered[-1:]):
            if group:
                out = correlate(place, [m for members in group for m in members], q_block, scale, out)
        return out

    return body


def solution(mesh):
    in_specs = (P("frames", "pix"), P("pix"), P("pix"), P("pix"), P("pix"))
    out_specs = P("frames", None, "pix", None)
    body = make_body(mesh)

    return jax.shard_map(body, mesh=mesh, in_specs=in_specs, out_specs=out_specs, check_vma=False)
```
